32 devices in a mesh: lat: 4 (over z), lon: 8 (over y, x, core).
Axes of the slice: x: 2, y: 2, z: 4, core: 2. Of those that a mesh axis runs over, the one named last changes fastest.
Arguments:
- grid_feats: float32 [4, 16, 128, 1024], P('lat', 'lon'), may hold values from -6 to 6
- lift_index: int32 [4, 24, 4], P('lat', 'lon'), may hold values from 0 to 63, as said below
- lift_weight: float32 [4, 24, 4, 128, 128], P('lat', 'lon'), may hold values from -0.25 to 0.25
- window_index: int32 [4, 24, 8], P('lat', 'lon'), may hold values from 0 to 95, as said below
- window_count: int32 [4, 24], P('lat', 'lon'), may hold values from 4 to 8
- norm_gains: float32 [2, 1024], replicated, may hold values from 0.5 to 1.5
- qkv_weight: bfloat16 [1024, 3072], replicated, may hold values from -6.5 to 6.5
- out_weight: bfloat16 [1024, 1024], replicated, may hold values from -0.1875 to 0.1875
- up_weight: bfloat16 [1024, 2048], replicated, may hold values from -0.1875 to 0.1875
- down_weight: bfloat16 [2048, 1024], replicated, may hold values from -0.125 to 0.125
- return_index: int32 [4, 16, 4], P('lat', 'lon'), may hold values from 0 to 95, as said below
- return_weight: float32 [4, 16, 4, 128, 128], P('lat', 'lon'), may hold values from -0.25 to 0.25
Outputs:
- grid_out: float32 [4, 16, 128, 1024], P('lat', 'lon')
The draws below stay inside these ranges and needn't reach their ends.
Inputs may be any that keep to these rules, and one draw needn't show every extreme that they name: `lift_index`: entries name grid blocks a' * 16 + b'; the 4 entries of a row differ; for mesh block (a, c), |a' - a| <= 1 and b' lies among the 4 columns from c // 3 * 2 - 1 to c // 3 * 2 + 2, counted modulo 16. `window_index`: entries name mesh blocks a' * 24 + c'; slot 0 is the query block itself, the 8 entries of a row differ; |a' - a| <= 1 and c' lies among the 5 columns from c // 3 * 3 - 1 to c // 3 * 3 + 3, counted modulo 24. `return_index`: entries name mesh blocks a' * 24 + c'; the 4 entries of a row differ; for grid block (a, b), |a' - a| <= 1 and c' lies among the 5 columns from b // 2 * 3 - 1 to b // 2 * 3 + 3, counted modulo 24.
All inputs are finite; a program needn't handle non-finite values.
Results may differ from the reference program's by a relative error of at most 0.0035.
Values may be sent and summed in bfloat16 or wider, within the bound.
A program may use at most 128 MiB of HBM per device.

```python
import jax
import jax.numpy as jnp
from jax import lax

HEADS = 16
C = 1024
FF = 2048
BLK = 128
K = 4
NW = 8
GLON = 2
MLON = 3
BANDS = 4
GRID_LON = 16
MESH_LON = 24


def pick_blocks(seed_key, target_lon, target_blocks, source_lon, source_blocks, pick_count, skip_self):
    across = source_blocks + 2
    band_index = jnp.arange(BANDS, dtype=jnp.int32).reshape(BANDS, 1, 1, 1)
    column_index = jnp.arange(target_lon, dtype=jnp.int32).reshape(1, target_lon, 1, 1)
    sector_index = column_index // target_blocks
    lat_step = jnp.arange(3, dtype=jnp.int32).reshape(1, 1, 3, 1)
    lon_step = jnp.arange(across, dtype=jnp.int32).reshape(1, 1, 1, across)
    source_band = band_index + lat_step - 1
    source_column = (sector_index * source_blocks + lon_step - 1) % source_lon
    usable = jnp.logical_and(source_band >= 0, source_band < BANDS)
    if skip_self:
        itself = jnp.logical_and(source_band == band_index, source_column == column_index)
        usable = jnp.logical_and(usable, jnp.logical_not(itself))
    full_shape = (BANDS, target_lon, 3, across)
    identity = jnp.broadcast_to(source_band * source_lon + source_column, full_shape)
    ordinal = jnp.broadcast_to(lat_step * across + lon_step, full_shape)
    jitter = jax.random.randint(seed_key, full_shape, 0, 1048576, dtype=jnp.int32)
    scores = jnp.where(usable, jitter * 64 + ordinal, -1)
    scores = scores.reshape(BANDS, target_lon, 3 * across)
    identity = identity.reshape(BANDS, target_lon, 3 * across)
    chosen_values, chosen_places = lax.top_k(scores, pick_count)
    return jnp.take_along_axis(identity, chosen_places, axis=-1).astype(jnp.int32)


def draw_lift_index(key, part):
    return pick_blocks(jax.random.fold_in(key, 11), MESH_LON, MLON, GRID_LON, GLON, K, False)


def draw_return_index(key, part):
    return pick_blocks(jax.random.fold_in(key, 12), GRID_LON, GLON, MESH_LON, MLON, K, False)


def draw_window_index(key, part):
    others = pick_blocks(jax.random.fold_in(key, 13), MESH_LON, MLON, MESH_LON, MLON, NW - 1, True)
    band_index = jnp.arange(BANDS, dtype=jnp.int32).reshape(BANDS, 1, 1)
    column_index = jnp.arange(MESH_LON, dtype=jnp.int32).reshape(1, MESH_LON, 1)
    itself = band_index * MESH_LON + column_index
    return jnp.concatenate([itself, others], axis=-1).astype(jnp.int32)


def draw_qkv_weight(key, part):
    standard = jnp.clip(jax.random.normal(jax.random.fold_in(key, 20), (C, 3 * C), dtype=jnp.float32), -6.0, 6.0) / jnp.sqrt(float(C))
    query_part = standard[:, :C] * 1.4
    value_part = standard[:, 2 * C:]
    key_part = standard[:, C:2 * C] * 1.4
    return jnp.concatenate([query_part, key_part, value_part], axis=1).astype(jnp.bfloat16)


def place_ends(array, stream_key, least, top_value):
    longest = array.shape.index(max(array.shape))
    spots = []
    for shift in (0, 1):
        where = [jax.random.randint(jax.random.fold_in(stream_key, axis), (), 0, length) for axis, length in enumerate(array.shape)]
        where[longest] = (where[longest] + shift) % array.shape[longest]
        spots.append(tuple(where))
    return array.at[spots[0]].set(least).at[spots[1]].set(top_value)


def block_scale(key, shape, shards, least, high):
    factor_of, own = 1.0, jax.random.fold_in(key, 6)
    for dim, blocks in shards:
        heights = jnp.exp(jax.random.uniform(jax.random.fold_in(own, dim), (blocks,), jnp.float32, least / len(shards), high / len(shards)))
        factor_of = factor_of * jnp.repeat(heights, shape[dim] // blocks).reshape([-1 if axis == dim else 1 for axis in range(len(shape))])
    return factor_of


def normal_values(rng, shape, scale, most, shards=(), held_as=jnp.bfloat16):
    result = jax.random.normal(rng, shape, jnp.float32) * scale
    if len(shards) > 0:
        result = block_scale(rng, shape, shards, -0.22, 0.18) * result
    return jnp.clip(result, min=-most, max=most).astype(held_as)


def setup_inputs(seed: int = 0) -> dict:
    arg_keys = jax.random.split(jax.random.key(seed), 13)
    return {
        "grid_feats": normal_values(arg_keys[0], (BANDS, GRID_LON, BLK, C), 1.0, 6.0, ((0, 4), (1, 8)), jnp.float32),
        "lift_index": draw_lift_index(jax.random.fold_in(arg_keys[12], 71), 0),
        "lift_weight": normal_values(arg_keys[2], (BANDS, MESH_LON, K, BLK, BLK), (K * BLK) ** -0.5, 0.25, ((0, 4), (1, 8)), jnp.float32),
        "window_index": draw_window_index(jax.random.fold_in(arg_keys[12], 71), 0),
        "window_count": place_ends(jax.random.randint(arg_keys[4], (BANDS, MESH_LON), NW // 2, NW + 1), jax.random.fold_in(arg_keys[4], 1), NW // 2, NW).astype(jnp.int32),
        "norm_gains": jnp.clip(1.0 + 0.1 * jax.random.normal(arg_keys[5], (2, C), jnp.float32), 0.5, 1.5),
        "qkv_weight": draw_qkv_weight(jax.random.fold_in(arg_keys[12], 71), 0),
        "out_weight": normal_values(arg_keys[7], (C, C), C ** -0.5, 0.1875),
        "up_weight": normal_values(arg_keys[8], (C, FF), C ** -0.5, 0.1875),
        "down_weight": normal_values(arg_keys[9], (FF, C), FF ** -0.5, 0.125),
        "return_index": draw_return_index(jax.random.fold_in(arg_keys[12], 71), 0),
        "return_weight": normal_values(arg_keys[11], (BANDS, GRID_LON, K, BLK, BLK), (K * BLK) ** -0.5, 0.25, ((0, 4), (1, 8)), jnp.float32),
    }


EPSILON = 1e-05

def layer_norm(values, gain):
    centred = values - lax.optimization_barrier(jnp.mean(values, axis=-1, keepdims=True))
    spread = lax.optimization_barrier(jnp.mean(centred * centred, axis=-1, keepdims=True))
    return (centred * lax.rsqrt(spread + EPSILON) * gain).astype(jnp.bfloat16)

def gelu_exact(values):
    return 0.5 * values * (1.0 + lax.erf(values * 0.7071067811865476))

def reference(grid_feats, lift_index, lift_weight, window_index, window_count, norm_gains, qkv_weight, out_weight, up_weight, down_weight, return_index, return_weight):
    feature_width = grid_feats.shape[-1]
    head_size = feature_width // HEADS
    grid_table = grid_feats.reshape(-1, BLK, feature_width)

    def lift_block(pair):
        slots, weight = pair
        return jnp.einsum('krs,ksc->rc', weight, grid_table[slots], precision=lax.Precision.HIGHEST)
    mesh_in = lax.map(lift_block, (lift_index.reshape(-1, K), lift_weight.reshape(-1, K, BLK, BLK)))
    normed = layer_norm(mesh_in, norm_gains[0]).reshape(-1, feature_width)
    projected = jnp.dot(normed, qkv_weight, preferred_element_type=jnp.float32).astype(jnp.bfloat16)
    projected = projected.reshape(-1, BLK, 3 * feature_width)

    def attend_block(triple):
        query_rows, slots, live_count = triple
        gathered = projected[slots]
        keys = gathered[:, :, feature_width:2 * feature_width].reshape(NW * BLK, HEADS, head_size).astype(jnp.float32)
        values = gathered[:, :, 2 * feature_width:].reshape(NW * BLK, HEADS, head_size).astype(jnp.float32)
        queries = query_rows[:, :feature_width].reshape(BLK, HEADS, head_size).astype(jnp.float32)
        scores = jnp.einsum('qhd,khd->hqk', queries, keys) * head_size ** (-0.5)
        live = jnp.arange(NW * BLK, dtype=jnp.int32) // BLK < live_count
        masked = jnp.where(live[None, None, :], scores, -1e+30)
        highest = lax.optimization_barrier(jnp.max(masked, axis=-1, keepdims=True))
        raw_weights = jnp.exp(masked - highest)
        weights = (raw_weights / lax.optimization_barrier(jnp.sum(raw_weights, axis=-1, keepdims=True))).astype(jnp.bfloat16)
        mixed_rows = jnp.einsum('hqk,khd->qhd', weights.astype(jnp.float32), values)
        return mixed_rows.astype(jnp.bfloat16).reshape(BLK, feature_width)
    mixed = lax.map(attend_block, (projected, window_index.reshape(-1, NW), window_count.reshape(-1)))
    mixed = mixed.reshape(-1, feature_width)
    after_attention = mesh_in.reshape(-1, feature_width) + jnp.dot(mixed, out_weight, preferred_element_type=jnp.float32)
    normed_again = layer_norm(after_attention, norm_gains[1])
    hidden_units = gelu_exact(jnp.dot(normed_again, up_weight, preferred_element_type=jnp.float32)).astype(jnp.bfloat16)
    mesh_out = after_attention + jnp.dot(hidden_units, down_weight, preferred_element_type=jnp.float32)
    mesh_table = mesh_out.reshape(-1, BLK, feature_width)

    def return_block(pair):
        slots, weight = pair
        return jnp.einsum('krs,ksc->rc', weight, mesh_table[slots], precision=lax.Precision.HIGHEST)
    grid_out = lax.map(return_block, (return_index.reshape(-1, K), return_weight.reshape(-1, K, BLK, BLK)))
    return grid_out.reshape(BANDS, GRID_LON, BLK, feature_width)
```

```python
import jax
import jax.numpy as jnp
from jax import lax
from jax.experimental import pallas as pl
from jax.experimental.pallas import tpu as pltpu
from jax.sharding import PartitionSpec as P

HEADS = 16


EPSILON = 1e-05

MESH = pl.DeviceIdType.MESH
VMEM_LIMIT = 60 * 1024 * 1024


def layer_norm(values, gain):
    centred = values - jnp.mean(values, axis=-1, keepdims=True)
    spread = jnp.mean(centred * centred, axis=-1, keepdims=True)
    return (centred * lax.rsqrt(spread + EPSILON) * gain).astype(jnp.bfloat16)


def gelu_exact(values):
    return 0.5 * values * (1.0 + lax.erf(values * 0.7071067811865476))


def table_slot(row, column, blocks):
    if 1 <= column <= blocks:
        return row * blocks + column - 1
    return 3 * blocks + (1, 0, 2)[row] * 2 + (0 if column == 0 else 1)


def find_slot(global_id, total_lon, blocks):
    band_here = lax.axis_index("lat")
    sector_here = lax.axis_index("lon")
    row = global_id // total_lon - band_here + 1
    column = (global_id % total_lon - sector_here * blocks + 1 + total_lon) % total_lon
    side_row = jnp.where(row == 1, 0, jnp.where(row == 0, 1, 2))
    side = 3 * blocks + side_row * 2 + jnp.where(column == 0, 0, 1)
    inside = jnp.logical_and(column >= 1, column <= blocks)
    return jnp.where(inside, row * blocks + column - 1, side)


class Halo:
    def __init__(self, source, table, send_sem, recv_sem, blocks, rows):
        self.blocks = blocks
        lat_count, lon_count = lax.axis_size("lat"), lax.axis_size("lon")
        lat, lon = lax.axis_index("lat"), lax.axis_index("lon")
        self.above, self.below = lat > 0, lat < lat_count - 1
        self.right = (lat, lax.rem(lon + 1, lon_count))
        self.left = (lat, lax.rem(lon + lon_count - 1, lon_count))
        self.down = (lax.rem(lat + 1, lat_count), lon)
        self.up = (lax.rem(lat + lat_count - 1, lat_count), lon)

        def own(block):
            return source.at[block]

        def slot(row, column):
            return table.at[table_slot(row, column, blocks)]

        def copy(src, dst, number, device):
            return pltpu.make_async_remote_copy(
                src_ref=src,
                dst_ref=dst,
                send_sem=send_sem.at[number],
                recv_sem=recv_sem.at[number],
                device_id=device,
                device_id_type=MESH,
            )

        last = blocks - 1
        self.edges = [
            copy(own(last), slot(1, 0), 0, self.right),
            copy(own(0), slot(1, blocks + 1), 1, self.left),
        ]
        self.downs = [copy(own(j), slot(0, 1 + j), 2 + j, self.down) for j in range(blocks)]
        self.ups = [copy(own(j), slot(2, 1 + j), 2 + blocks + j, self.up) for j in range(blocks)]
        base = 2 + 2 * blocks
        self.corners_above = [
            copy(slot(0, blocks), slot(0, 0), base, self.right),
            copy(slot(0, 1), slot(0, blocks + 1), base + 1, self.left),
        ]
        self.corners_below = [
            copy(slot(2, blocks), slot(2, 0), base + 2, self.right),
            copy(slot(2, 1), slot(2, blocks + 1), base + 3, self.left),
        ]
        self.border = [0, last] if blocks > 1 else [0]
        self.middle = [j for j in range(blocks) if j not in self.border]

    @staticmethod
    def count(blocks):
        return 6 + 2 * blocks

    def greet(self):
        barrier = pltpu.get_barrier_semaphore()
        for device in (self.left, self.right):
            pl.semaphore_signal(barrier, inc=1, device_id=device, device_id_type=MESH)

        @pl.when(self.above)
        def _():
            pl.semaphore_signal(barrier, inc=1, device_id=self.up, device_id_type=MESH)

        @pl.when(self.below)
        def _():
            pl.semaphore_signal(barrier, inc=1, device_id=self.down, device_id_type=MESH)

        bands = self.above.astype(jnp.int32) + self.below.astype(jnp.int32)
        pl.semaphore_wait(barrier, 2 + bands)

    def start(self):
        for edge in self.edges:
            edge.start()
        for j in self.border + self.middle:
            @pl.when(self.below)
            def _():
                self.downs[j].start()

            @pl.when(self.above)
            def _():
                self.ups[j].start()

    def forward(self):
        @pl.when(self.above)
        def _():
            for j in self.border:
                self.downs[j].wait_recv()
            for corner in self.corners_above:
                corner.start()

        @pl.when(self.below)
        def _():
            for j in self.border:
                self.ups[j].wait_recv()
            for corner in self.corners_below:
                corner.start()

    def wait_edges(self):
        for edge in self.edges:
            edge.wait_recv()

    def wait_above(self):
        @pl.when(self.above)
        def _():
            for j in self.middle:
                self.downs[j].wait_recv()

    def wait_below(self):
        @pl.when(self.below)
        def _():
            for j in self.middle:
                self.ups[j].wait_recv()

    def wait_corners(self):
        @pl.when(self.above)
        def _():
            for corner in self.corners_above:
                corner.wait_recv()

        @pl.when(self.below)
        def _():
            for corner in self.corners_below:
                corner.wait_recv()

    def finish(self):
        for edge in self.edges:
            edge.wait_send()

        @pl.when(self.above)
        def _():
            for sent in self.ups + self.corners_above:
                sent.wait_send()

        @pl.when(self.below)
        def _():
            for sent in self.downs + self.corners_below:
                sent.wait_send()


def interpolate(slot_ref, weight_ref, table, target, rows):
    total = None
    for k in range(weight_ref.shape[1]):
        block = table[slot_ref[target, k]]
        weight = weight_ref[target, k]
        high = weight.astype(jnp.bfloat16)
        low = (weight - high.astype(jnp.float32)).astype(jnp.bfloat16)
        both = jnp.dot(
            jnp.concatenate([high, low], axis=0), block, preferred_element_type=jnp.float32
        )
        term = both[:rows] + both[rows:]
        total = term if total is None else total + term
    return total


def lift_kernel(
    blocks, rows,
    slot_ref, grid_ref, weight_ref, gain_ref, mesh_in_ref, normed_ref, table, send_sem, recv_sem,
):
    halo = Halo(grid_ref, table, send_sem, recv_sem, blocks, rows)
    halo.greet()
    halo.start()
    table[pl.ds(blocks, blocks)] = grid_ref[...]
    halo.forward()
    halo.wait_edges()
    halo.wait_above()
    halo.wait_below()
    halo.wait_corners()

    @pl.loop(0, weight_ref.shape[0])
    def _(target):
        total = interpolate(slot_ref, weight_ref, table, target, rows)
        mesh_in_ref[target] = total
        normed_ref[target] = layer_norm(total, gain_ref[0:1, :])

    halo.finish()


def return_kernel(
    blocks, rows,
    slot_ref, mesh_ref, weight_ref, out_ref, table, send_sem, recv_sem,
):
    halo = Halo(mesh_ref, table, send_sem, recv_sem, blocks, rows)
    halo.greet()
    halo.start()
    table[pl.ds(blocks, blocks)] = mesh_ref[...]
    halo.forward()
    halo.wait_edges()
    halo.wait_above()
    halo.wait_below()
    halo.wait_corners()

    @pl.loop(0, weight_ref.shape[0])
    def _(target):
        total = interpolate(slot_ref, weight_ref, table, target, rows)
        out_ref[target] = total

    halo.finish()


def attention_kernel(
    blocks, rows, tile,
    slot_ref, count_ref, normed_ref, weight_ref, mixed_ref,
    table, queries, key_value, send_sem, recv_sem,
):
    width = normed_ref.shape[2]
    pair = 2 * (width // HEADS)
    halo = Halo(normed_ref, table, send_sem, recv_sem, blocks, rows)
    halo.greet()
    halo.start()
    scale = (width // HEADS) ** (-0.5)

    @pl.loop(0, width // tile)
    def _(step):
        columns = pl.ds(pl.multiple_of(step * tile, tile), tile)
        product = jnp.dot(
            normed_ref[...].reshape(blocks * rows, width),
            weight_ref[:, columns],
            preferred_element_type=jnp.float32,
        )
        product = product.astype(jnp.bfloat16) * jnp.bfloat16(scale)
        queries[:, :, columns] = product.reshape(blocks, rows, tile)

    def project(source, first, many):
        @pl.loop(0, 2 * width // tile)
        def _(step):
            columns = pl.ds(pl.multiple_of(step * tile, tile), tile)
            taken = pl.ds(pl.multiple_of(width + step * tile, tile), tile)
            product = jnp.dot(
                source[...].reshape(many * rows, width),
                weight_ref[:, taken],
                preferred_element_type=jnp.float32,
            )
            product = product.astype(jnp.bfloat16).reshape(many, rows, tile)
            key_value[pl.ds(first, many), :, columns] = product

    def project_slots(first, many):
        project(table.at[pl.ds(first, many)], first, many)

    project(normed_ref, blocks, blocks)
    halo.wait_edges()
    halo.forward()
    project_slots(3 * blocks, 2)
    halo.wait_above()
    project_slots(0, blocks)
    halo.wait_below()
    project_slots(2 * blocks, blocks)
    halo.wait_corners()
    project_slots(3 * blocks + 2, 4)

    slots = slot_ref.shape[1]
    lane = lax.broadcasted_iota(jnp.int32, (rows, pair), 1)
    first_half = lane < pair // 2
    key_block = lax.broadcasted_iota(jnp.int32, (1, slots * rows), 1) // rows

    @pl.loop(0, blocks)
    def _(target):
        live = key_block < count_ref[0, target]
        places = [slot_ref[target, s] for s in range(slots)]

        @pl.loop(0, width // pair)
        def _(group):
            columns = pl.ds(pl.multiple_of(group * pair, pair), pair)
            value_columns = pl.ds(pl.multiple_of(width + group * pair, pair), pair)
            query = queries[target, :, columns]
            zero = jnp.zeros_like(query)
            both = jnp.concatenate(
                [jnp.where(first_half, query, zero), jnp.where(first_half, zero, query)], axis=0
            )
            keys = jnp.concatenate([key_value[place, :, columns] for place in places], axis=0)
            values = jnp.concatenate([key_value[place, :, value_columns] for place in places], axis=0)
            scores = lax.dot_general(
                both, keys, (((1,), (1,)), ((), ())), preferred_element_type=jnp.float32
            )
            masked = jnp.where(live, scores, -1e30)
            raw = jnp.exp(masked - jnp.max(masked, axis=-1, keepdims=True))
            total = jnp.sum(raw, axis=-1, keepdims=True)
            mixed = jnp.dot(
                raw.astype(jnp.bfloat16), values, preferred_element_type=jnp.float32
            ) / total
            mixed_ref[target, :, columns] = jnp.where(
                first_half, mixed[:rows], mixed[rows:]
            ).astype(jnp.bfloat16)

    halo.finish()


def in_vmem(count):
    return [pl.BlockSpec(memory_space=pltpu.VMEM)] * count


def in_smem(count):
    return [pl.BlockSpec(memory_space=pltpu.SMEM)] * count


def halo_scratch(blocks, rows, width):
    count = Halo.count(blocks)
    slots = 3 * (blocks + 2)
    return (
        [pltpu.VMEM((slots, rows, width), jnp.bfloat16)],
        [pltpu.SemaphoreType.DMA((count,)), pltpu.SemaphoreType.DMA((count,))],
    )


def parameters(number):
    return pltpu.CompilerParams(
        collective_id=number, has_side_effects=True, vmem_limit_bytes=VMEM_LIMIT
    )


def shards(
    grid_feats,
    lift_index,
    lift_weight,
    window_index,
    window_count,
    norm_gains,
    qkv_weight,
    out_weight,
    up_weight,
    down_weight,
    return_index,
    return_weight,
):
    lon_count = lax.axis_size("lon")
    grid_blocks = grid_feats.shape[1]
    mesh_blocks = lift_index.shape[1]
    rows = grid_feats.shape[2]
    width = grid_feats.shape[3]
    grid_lon = grid_blocks * lon_count
    mesh_lon = mesh_blocks * lon_count

    grid_table, grid_sems = halo_scratch(grid_blocks, rows, width)
    mesh_table, mesh_sems = halo_scratch(mesh_blocks, rows, width)
    mesh_in, normed = pl.pallas_call(
        lambda *refs: lift_kernel(grid_blocks, rows, *refs),
        out_shape=(
            jax.ShapeDtypeStruct((mesh_blocks, rows, width), jnp.float32),
            jax.ShapeDtypeStruct((mesh_blocks, rows, width), jnp.bfloat16),
        ),
        in_specs=in_smem(1) + in_vmem(3),
        out_specs=tuple(in_vmem(2)),
        scratch_shapes=grid_table + grid_sems,
        compiler_params=parameters(0),
    )(
        find_slot(lift_index[0], grid_lon, grid_blocks),
        grid_feats[0].astype(jnp.bfloat16),
        lift_weight[0],
        norm_gains,
    )
    tile = min(512, width)
    mixed = pl.pallas_call(
        lambda *refs: attention_kernel(mesh_blocks, rows, tile, *refs),
        out_shape=jax.ShapeDtypeStruct((mesh_blocks, rows, width), jnp.bfloat16),
        in_specs=in_smem(2) + in_vmem(2),
        out_specs=in_vmem(1)[0],
        scratch_shapes=mesh_table
        + [
            pltpu.VMEM((mesh_blocks, rows, width), jnp.bfloat16),
            pltpu.VMEM((3 * (mesh_blocks + 2), rows, 2 * width), jnp.bfloat16),
        ]
        + mesh_sems,
        compiler_params=parameters(1),
    )(find_slot(window_index[0], mesh_lon, mesh_blocks), window_count, normed, qkv_weight)
    mixed = mixed.reshape(-1, width)
    after_attention = mesh_in.reshape(-1, width) + jnp.dot(
        mixed, out_weight, preferred_element_type=jnp.float32
    )
    normed_again = layer_norm(after_attention, norm_gains[1])
    hidden_units = gelu_exact(
        jnp.dot(normed_again, up_weight, preferred_element_type=jnp.float32)
    ).astype(jnp.bfloat16)
    mesh_out = after_attention + jnp.dot(
        hidden_units, down_weight, preferred_element_type=jnp.float32
    )
    grid_out = pl.pallas_call(
        lambda *refs: return_kernel(mesh_blocks, rows, *refs),
        out_shape=jax.ShapeDtypeStruct((grid_blocks, rows, width), jnp.float32),
        in_specs=in_smem(1) + in_vmem(2),
        out_specs=in_vmem(1)[0],
        scratch_shapes=mesh_table + mesh_sems,
        compiler_params=parameters(2),
    )(
        find_slot(return_index[0], mesh_lon, mesh_blocks),
        mesh_out.astype(jnp.bfloat16).reshape(mesh_blocks, rows, width),
        return_weight[0],
    )
    return grid_out.reshape(1, grid_blocks, rows, width)


def solution(mesh):
    placed = (
        P("lat", "lon", None, None),
        P("lat", "lon", None),
        P("lat", "lon", None, None, None),
        P("lat", "lon", None),
        P("lat", "lon"),
        P(),
        P(),
        P(),
        P(),
        P(),
        P("lat", "lon", None),
        P("lat", "lon", None, None, None),
    )
    return jax.shard_map(
        shards, mesh=mesh, in_specs=placed, out_specs=P("lat", "lon", None, None), check_vma=False
    )
```

```python
import jax
import jax.numpy as jnp
from jax import lax
from jax.experimental import pallas as pl
from jax.experimental.pallas import tpu as pltpu
from jax.sharding import PartitionSpec as P

HEADS = 16


EPSILON = 1e-05

MESH = pl.DeviceIdType.MESH
VMEM_LIMIT = 60 * 1024 * 1024


def layer_norm(values, gain):
    centred = values - jnp.mean(values, axis=-1, keepdims=True)
    spread = jnp.mean(centred * centred, axis=-1, keepdims=True)
    return (centred * lax.rsqrt(spread + EPSILON) * gain).astype(jnp.bfloat16)


def gelu_exact(values):
    return 0.5 * values * (1.0 + lax.erf(values * 0.7071067811865476))


def find_slot(global_id, total_lon, blocks):
    sector_here = lax.axis_index("lon")
    odd = lax.rem(sector_here, 2)
    source_band = lax.div(global_id, total_lon)
    row = source_band - lax.axis_index("lat")
    column = lax.rem(
        global_id - source_band * total_lon - sector_here * blocks + 1 + total_lon, total_lon
    )
    band = jnp.where(row < 0, 0, 1)
    place = column - 1
    side = jnp.where(column == 0, 0, 1)
    outside = jnp.logical_or(column == 0, column == blocks + 1)
    first = odd * (blocks - 1)
    corner = jnp.where(side == odd, blocks + 8 + 2 * (blocks - 2) + band, blocks + 6 + band)
    border = jnp.where(place == first, blocks + 2 + band, blocks + 4 + band)
    between = blocks + 8 + band * (blocks - 2) + place - 1
    middle = jnp.logical_and(place > 0, place < blocks - 1)
    other = jnp.where(outside, corner, jnp.where(middle, between, border))
    same = jnp.where(outside, blocks + side, place)
    found = jnp.where(row == 0, same, other)
    return jnp.minimum(jnp.maximum(found, 0), 3 * (blocks + 2) - 1)


class Halo:
    def __init__(self, source, table, send_sem, recv_sem, blocks):
        lat_count, lon_count = lax.axis_size("lat"), lax.axis_size("lon")
        lat, lon = lax.axis_index("lat"), lax.axis_index("lon")
        odd = lax.rem(lon, 2)
        self.above, self.below = lat > 0, lat < lat_count - 1
        self.outer = (lat, lax.rem(lon + 2 * odd - 1 + lon_count, lon_count))
        self.inner = (lat, lax.rem(lon + 1 - 2 * odd + lon_count, lon_count))
        self.down = (lax.rem(lat + 1, lat_count), lon)
        self.up = (lax.rem(lat + lat_count - 1, lat_count), lon)
        first = odd * (blocks - 1)
        second = blocks - 1 - first
        number = 0

        def copy(src, dst, device):
            nonlocal number
            number += 1
            return pltpu.make_async_remote_copy(
                src_ref=src,
                dst_ref=dst,
                send_sem=send_sem.at[number - 1],
                recv_sem=recv_sem.at[number - 1],
                device_id=device,
                device_id_type=MESH,
            )

        self.edges = [
            copy(source.at[first], table.at[blocks + 1 - odd], self.outer),
            copy(source.at[second], table.at[blocks + odd], self.inner),
        ]
        ends = [(first, blocks + 2), (second, blocks + 4)]
        self.vertical = []
        for place, slot in ends:
            self.vertical.append(
                (
                    copy(source.at[place], table.at[slot], self.down),
                    copy(source.at[place], table.at[slot + 1], self.up),
                )
            )
        between = blocks + 8
        for place in range(1, blocks - 1):
            slot = between + place - 1
            self.vertical.append(
                (
                    copy(source.at[place], table.at[slot], self.down),
                    copy(source.at[place], table.at[slot + blocks - 2], self.up),
                )
            )
        last = between + 2 * (blocks - 2)
        self.corners = [
            [
                copy(table.at[blocks + 2 + band], table.at[last + band], self.outer)
                for band in (0, 1)
            ],
            [
                copy(table.at[blocks + 4 + band], table.at[blocks + 6 + band], self.inner)
                for band in (0, 1)
            ],
        ]

    @staticmethod
    def count(blocks):
        return 6 + 2 * blocks

    def greet(self):
        barrier = pltpu.get_barrier_semaphore()
        for device in (self.outer, self.inner):
            pl.semaphore_signal(barrier, inc=1, device_id=device, device_id_type=MESH)

        @pl.when(self.above)
        def _():
            pl.semaphore_signal(barrier, inc=1, device_id=self.up, device_id_type=MESH)

        @pl.when(self.below)
        def _():
            pl.semaphore_signal(barrier, inc=1, device_id=self.down, device_id_type=MESH)

        bands = self.above.astype(jnp.int32) + self.below.astype(jnp.int32)
        pl.semaphore_wait(barrier, 2 + bands)

    def start(self):
        for edge in self.edges[:1]:
            edge.start()
        for down, up in self.vertical:
            @pl.when(self.below)
            def _():
                down.start()

            @pl.when(self.above)
            def _():
                up.start()
        for edge in self.edges[1:]:
            edge.start()

    def forward(self, order):
        down, up = self.vertical[order]
        above, below = self.corners[order]

        @pl.when(self.above)
        def _():
            down.wait_recv()
            above.start()

        @pl.when(self.below)
        def _():
            up.wait_recv()
            below.start()

    def wait_edges(self):
        for edge in self.edges:
            edge.wait_recv()

    def wait_corners(self, order):
        above, below = self.corners[order]

        @pl.when(self.above)
        def _():
            above.wait_recv()

        @pl.when(self.below)
        def _():
            below.wait_recv()

    def wait_between(self):
        for down, up in self.vertical[2:]:
            @pl.when(self.above)
            def _():
                down.wait_recv()

            @pl.when(self.below)
            def _():
                up.wait_recv()

    def receive(self, blocks, work):
        self.forward(0)
        self.wait_edges()
        work(blocks, 4)
        self.forward(1)
        self.wait_corners(1)
        work(blocks + 4, 4)
        self.wait_between()
        self.wait_corners(0)
        work(blocks + 8, 2 * (blocks - 2) + 2)

    def finish(self):
        for edge in self.edges:
            edge.wait_send()

        @pl.when(self.above)
        def _():
            for _, up in self.vertical:
                up.wait_send()
            for above, _ in self.corners:
                above.wait_send()

        @pl.when(self.below)
        def _():
            for down, _ in self.vertical:
                down.wait_send()
            for _, below in self.corners:
                below.wait_send()


SPREAD = 20.0


def encode(values):
    return jnp.exp2(values * SPREAD).astype(jnp.bfloat16)


def decode(coded):
    return jnp.log2(coded.astype(jnp.float32)) * (1.0 / SPREAD)


def halves(values):
    high = values.astype(jnp.bfloat16)
    low = (values - high.astype(jnp.float32)).astype(jnp.bfloat16)
    return high, low


def lift_kernel(
    total_lon, blocks, rows,
    index_ref, grid_ref, weight_ref, gain_ref, mesh_in_ref, normed_ref,
    table, high_table, low_table, send_sem, recv_sem,
):
    halo = Halo(grid_ref, table, send_sem, recv_sem, blocks)
    halo.greet()
    halo.start()

    def unpack(source, start, first, many):
        @pl.loop(0, many)
        def _(block):
            high, low = halves(decode(source[start + block]))
            high_table[first + block] = high
            low_table[first + block] = low

    unpack(grid_ref, 0, 0, blocks)
    halo.receive(blocks, lambda first, many: unpack(table, first, first, many))

    @pl.loop(0, weight_ref.shape[0])
    def _(target):
        total = None
        for k in range(weight_ref.shape[1]):
            place = find_slot(index_ref[target, k], total_lon, blocks)
            high, low = halves(weight_ref[target, k])
            both = jnp.dot(
                jnp.concatenate([high, low], axis=0),
                high_table[place],
                preferred_element_type=jnp.float32,
            )
            rest = jnp.dot(high, low_table[place], preferred_element_type=jnp.float32)
            term = both[:rows] + (both[rows:] + rest)
            total = term if total is None else total + term
        mesh_in_ref[target] = total
        normed_ref[target] = layer_norm(total, gain_ref[0:1, :])

    halo.finish()


def return_kernel(
    total_lon, blocks, rows,
    index_ref, mesh_ref, weight_ref, out_ref, table, send_sem, recv_sem,
):
    halo = Halo(mesh_ref, table, send_sem, recv_sem, blocks)
    halo.greet()
    halo.start()
    table[pl.ds(0, blocks)] = mesh_ref[...]
    halo.receive(blocks, lambda first, many: None)

    @pl.loop(0, weight_ref.shape[0])
    def _(target):
        total = None
        for k in range(weight_ref.shape[1]):
            place = find_slot(index_ref[target, k], total_lon, blocks)
            high, low = halves(weight_ref[target, k])
            both = jnp.dot(
                jnp.concatenate([high, low], axis=0),
                table[place],
                preferred_element_type=jnp.float32,
            )
            term = both[:rows] + both[rows:]
            total = term if total is None else total + term
        out_ref[target] = total

    halo.finish()


def attention_kernel(
    total_lon, blocks, rows, tile,
    index_ref, count_ref, normed_ref, weight_ref, mixed_ref,
    table, queries, key_value, send_sem, recv_sem,
):
    width = normed_ref.shape[2]
    pair = 2 * (width // HEADS)
    halo = Halo(normed_ref, table, send_sem, recv_sem, blocks)
    halo.greet()
    halo.start()
    scale = (width // HEADS) ** (-0.5)

    @pl.loop(0, width // tile)
    def _(step):
        columns = pl.ds(pl.multiple_of(step * tile, tile), tile)
        product = jnp.dot(
            normed_ref[...].reshape(blocks * rows, width),
            weight_ref[:, columns],
            preferred_element_type=jnp.float32,
        )
        product = product.astype(jnp.bfloat16) * jnp.bfloat16(scale)
        queries[:, :, columns] = product.reshape(blocks, rows, tile)

    def project(source, first, many):
        @pl.loop(0, 2 * width // tile)
        def _(step):
            columns = pl.ds(pl.multiple_of(step * tile, tile), tile)
            taken = pl.ds(pl.multiple_of(width + step * tile, tile), tile)
            product = jnp.dot(
                source[...].reshape(many * rows, width),
                weight_ref[:, taken],
                preferred_element_type=jnp.float32,
            )
            product = product.astype(jnp.bfloat16).reshape(many, rows, tile)
            key_value[pl.ds(first, many), :, columns] = product

    def project_slots(first, many):
        project(table.at[pl.ds(first, many)], first, many)

    project(normed_ref, 0, blocks)
    halo.receive(blocks, project_slots)

    slots = index_ref.shape[1]
    lane = lax.broadcasted_iota(jnp.int32, (rows, pair), 1)
    first_half = lane < pair // 2
    key_block = lax.broadcasted_iota(jnp.int32, (1, slots * rows), 1) // rows

    @pl.loop(0, blocks)
    def _(target):
        live = key_block < count_ref[0, target]
        places = [find_slot(index_ref[target, s], total_lon, blocks) for s in range(slots)]

        def attend(group):
            columns = pl.ds(pl.multiple_of(group * pair, pair), pair)
            value_columns = pl.ds(pl.multiple_of(width + group * pair, pair), pair)
            query = queries[target, :, columns]
            zero = jnp.zeros_like(query)
            both = jnp.concatenate(
                [jnp.where(first_half, query, zero), jnp.where(first_half, zero, query)], axis=0
            )
            keys = jnp.concatenate([key_value[place, :, columns] for place in places], axis=0)
            values = jnp.concatenate([key_value[place, :, value_columns] for place in places], axis=0)
            scores = lax.dot_general(
                both, keys, (((1,), (1,)), ((), ())), preferred_element_type=jnp.float32
            )
            masked = jnp.where(live, scores, -1e30)
            raw = jnp.exp(masked - jnp.max(masked, axis=-1, keepdims=True))
            total = jnp.sum(raw, axis=-1, keepdims=True)
            mixed = jnp.dot(
                raw.astype(jnp.bfloat16), values, preferred_element_type=jnp.float32
            ) / total
            mixed_ref[target, :, columns] = jnp.where(
                first_half, mixed[:rows], mixed[rows:]
            ).astype(jnp.bfloat16)

        @pl.loop(0, width // pair // 2)
        def _(step):
            attend(2 * step)
            attend(2 * step + 1)

    halo.finish()


def in_vmem(count):
    return [pl.BlockSpec(memory_space=pltpu.VMEM)] * count


def in_smem(count):
    return [pl.BlockSpec(memory_space=pltpu.SMEM)] * count


def halo_scratch(blocks, rows, width):
    count = Halo.count(blocks)
    slots = 3 * (blocks + 2)
    return (
        [pltpu.VMEM((slots, rows, width), jnp.bfloat16)],
        [pltpu.SemaphoreType.DMA((count,)), pltpu.SemaphoreType.DMA((count,))],
    )


def parameters(number):
    return pltpu.CompilerParams(
        collective_id=number, has_side_effects=True, vmem_limit_bytes=VMEM_LIMIT
    )


def shards(
    grid_feats,
    lift_index,
    lift_weight,
    window_index,
    window_count,
    norm_gains,
    qkv_weight,
    out_weight,
    up_weight,
    down_weight,
    return_index,
    return_weight,
):
    lon_count = lax.axis_size("lon")
    grid_blocks = grid_feats.shape[1]
    mesh_blocks = lift_index.shape[1]
    rows = grid_feats.shape[2]
    width = grid_feats.shape[3]
    grid_lon = grid_blocks * lon_count
    mesh_lon = mesh_blocks * lon_count

    grid_table, grid_sems = halo_scratch(grid_blocks, rows, width)
    mesh_table, mesh_sems = halo_scratch(mesh_blocks, rows, width)
    mesh_in, normed = pl.pallas_call(
        lambda *refs: lift_kernel(grid_lon, grid_blocks, rows, *refs),
        out_shape=(
            jax.ShapeDtypeStruct((mesh_blocks, rows, width), jnp.float32),
            jax.ShapeDtypeStruct((mesh_blocks, rows, width), jnp.bfloat16),
        ),
        in_specs=in_smem(1) + in_vmem(3),
        out_specs=tuple(in_vmem(2)),
        scratch_shapes=grid_table * 3 + grid_sems,
        compiler_params=parameters(0),
    )(
        lift_index[0],
        encode(grid_feats[0]),
        lift_weight[0],
        norm_gains,
    )
    tile = min(512, width)
    mixed = pl.pallas_call(
        lambda *refs: attention_kernel(mesh_lon, mesh_blocks, rows, tile, *refs),
        out_shape=jax.ShapeDtypeStruct((mesh_blocks, rows, width), jnp.bfloat16),
        in_specs=in_smem(2) + in_vmem(2),
        out_specs=in_vmem(1)[0],
        scratch_shapes=mesh_table
        + [
            pltpu.VMEM((mesh_blocks, rows, width), jnp.bfloat16),
            pltpu.VMEM((3 * (mesh_blocks + 2), rows, 2 * width), jnp.bfloat16),
        ]
        + mesh_sems,
        compiler_params=parameters(1),
    )(window_index[0], window_count, normed, qkv_weight)
    mixed = mixed.reshape(-1, width)
    after_attention = mesh_in.reshape(-1, width) + jnp.dot(
        mixed, out_weight, preferred_element_type=jnp.float32
    )
    normed_again = layer_norm(after_attention, norm_gains[1])
    hidden_units = gelu_exact(
        jnp.dot(normed_again, up_weight, preferred_element_type=jnp.float32)
    ).astype(jnp.bfloat16)
    mesh_out = after_attention + jnp.dot(
        hidden_units, down_weight, preferred_element_type=jnp.float32
    )
    grid_out = pl.pallas_call(
        lambda *refs: return_kernel(mesh_lon, mesh_blocks, rows, *refs),
        out_shape=jax.ShapeDtypeStruct((grid_blocks, rows, width), jnp.float32),
        in_specs=in_smem(1) + in_vmem(2),
        out_specs=in_vmem(1)[0],
        scratch_shapes=mesh_table + mesh_sems,
        compiler_params=parameters(2),
    )(
        return_index[0],
        mesh_out.astype(jnp.bfloat16).reshape(mesh_blocks, rows, width),
        return_weight[0],
    )
    return grid_out.reshape(1, grid_blocks, rows, width)


def solution(mesh):
    placed = (
        P("lat", "lon", None, None),
        P("lat", "lon", None),
        P("lat", "lon", None, None, None),
        P("lat", "lon", None),
        P("lat", "lon"),
        P(),
        P(),
        P(),
        P(),
        P(),
        P("lat", "lon", None),
        P("lat", "lon", None, None, None),
    )
    return jax.shard_map(
        shards, mesh=mesh, in_specs=placed, out_specs=P("lat", "lon", None, None), check_vma=False
    )
```

```python
import jax
import jax.numpy as jnp
from jax import lax
from jax.experimental import pallas as pl
from jax.experimental.pallas import tpu as pltpu
from jax.sharding import PartitionSpec as P

HEADS = 16


EPSILON = 1e-05

MESH = pl.DeviceIdType.MESH
VMEM_LIMIT = 60 * 1024 * 1024


def layer_norm(values, gain):
    centred = values - jnp.mean(values, axis=-1, keepdims=True)
    spread = jnp.mean(centred * centred, axis=-1, keepdims=True)
    return (centred * lax.rsqrt(spread + EPSILON) * gain).astype(jnp.bfloat16)


def gelu_exact(values):
    return 0.5 * values * (1.0 + lax.erf(values * 0.7071067811865476))


def find_slot(global_id, total_lon, blocks):
    sector_here = lax.axis_index("lon")
    odd = lax.rem(sector_here, 2)
    source_band = lax.div(global_id, total_lon)
    row = source_band - lax.axis_index("lat")
    column = lax.rem(
        global_id - source_band * total_lon - sector_here * blocks + 1 + total_lon, total_lon
    )
    band = jnp.where(row < 0, 0, 1)
    place = column - 1
    side = jnp.where(column == 0, 0, 1)
    outside = jnp.logical_or(column == 0, column == blocks + 1)
    first = odd * (blocks - 1)
    corner = jnp.where(side == odd, blocks + 8 + 2 * (blocks - 2) + band, blocks + 6 + band)
    border = jnp.where(place == first, blocks + 2 + band, blocks + 4 + band)
    between = blocks + 8 + band * (blocks - 2) + place - 1
    middle = jnp.logical_and(place > 0, place < blocks - 1)
    other = jnp.where(outside, corner, jnp.where(middle, between, border))
    same = jnp.where(outside, blocks + side, place)
    found = jnp.where(row == 0, same, other)
    return jnp.minimum(jnp.maximum(found, 0), 3 * (blocks + 2) - 1)


class Halo:
    def __init__(self, source, table, send_sem, recv_sem):
        blocks = source.shape[0]
        lat_count, lon_count = lax.axis_size("lat"), lax.axis_size("lon")
        lat, lon = lax.axis_index("lat"), lax.axis_index("lon")
        odd = lax.rem(lon, 2)
        self.above, self.below = lat > 0, lat < lat_count - 1
        self.outer = (lat, lax.rem(lon + 2 * odd - 1 + lon_count, lon_count))
        self.inner = (lat, lax.rem(lon + 1 - 2 * odd + lon_count, lon_count))
        self.down = (lax.rem(lat + 1, lat_count), lon)
        self.up = (lax.rem(lat + lat_count - 1, lat_count), lon)
        first = odd * (blocks - 1)
        second = blocks - 1 - first
        number = 0

        def copy(src, dst, device):
            nonlocal number
            number += 1
            return pltpu.make_async_remote_copy(
                src_ref=src,
                dst_ref=dst,
                send_sem=send_sem.at[number - 1],
                recv_sem=recv_sem.at[number - 1],
                device_id=device,
                device_id_type=MESH,
            )

        self.edges = [
            copy(source.at[first], table.at[blocks + 1 - odd], self.outer),
            copy(source.at[second], table.at[blocks + odd], self.inner),
        ]
        ends = [(first, blocks + 2), (second, blocks + 4)]
        self.vertical = []
        for place, slot in ends:
            self.vertical.append(
                (
                    copy(source.at[place], table.at[slot], self.down),
                    copy(source.at[place], table.at[slot + 1], self.up),
                )
            )
        between = blocks + 8
        for place in range(1, blocks - 1):
            slot = between + place - 1
            self.vertical.append(
                (
                    copy(source.at[place], table.at[slot], self.down),
                    copy(source.at[place], table.at[slot + blocks - 2], self.up),
                )
            )
        last = between + 2 * (blocks - 2)
        self.corners = [
            [
                copy(table.at[blocks + 2 + band], table.at[last + band], self.outer)
                for band in (0, 1)
            ],
            [
                copy(table.at[blocks + 4 + band], table.at[blocks + 6 + band], self.inner)
                for band in (0, 1)
            ],
        ]

    @staticmethod
    def count(blocks):
        return 6 + 2 * blocks

    def greet(self):
        barrier = pltpu.get_barrier_semaphore()
        for device in (self.outer, self.inner):
            pl.semaphore_signal(barrier, inc=1, device_id=device, device_id_type=MESH)

        @pl.when(self.above)
        def _():
            pl.semaphore_signal(barrier, inc=1, device_id=self.up, device_id_type=MESH)

        @pl.when(self.below)
        def _():
            pl.semaphore_signal(barrier, inc=1, device_id=self.down, device_id_type=MESH)

        bands = self.above.astype(jnp.int32) + self.below.astype(jnp.int32)
        pl.semaphore_wait(barrier, 2 + bands)

    def start(self):
        for edge in self.edges[:1]:
            edge.start()
        for down, up in self.vertical:
            @pl.when(self.below)
            def _():
                down.start()

            @pl.when(self.above)
            def _():
                up.start()
        for edge in self.edges[1:]:
            edge.start()

    def forward(self, order):
        down, up = self.vertical[order]
        above, below = self.corners[order]

        @pl.when(self.above)
        def _():
            down.wait_recv()
            above.start()

        @pl.when(self.below)
        def _():
            up.wait_recv()
            below.start()

    def wait_edges(self):
        for edge in self.edges:
            edge.wait_recv()

    def wait_corners(self, order):
        above, below = self.corners[order]

        @pl.when(self.above)
        def _():
            above.wait_recv()

        @pl.when(self.below)
        def _():
            below.wait_recv()

    def wait_between(self):
        for down, up in self.vertical[2:]:
            @pl.when(self.above)
            def _():
                down.wait_recv()

            @pl.when(self.below)
            def _():
                up.wait_recv()

    def receive(self, blocks, work):
        self.forward(0)
        self.wait_edges()
        work(blocks, 4)
        self.forward(1)
        self.wait_corners(1)
        work(blocks + 4, 4)
        self.wait_between()
        self.wait_corners(0)
        work(blocks + 8, 2 * (blocks - 2) + 2)

    def finish(self):
        for edge in self.edges:
            edge.wait_send()

        @pl.when(self.above)
        def _():
            for _, up in self.vertical:
                up.wait_send()
            for above, _ in self.corners:
                above.wait_send()

        @pl.when(self.below)
        def _():
            for down, _ in self.vertical:
                down.wait_send()
            for _, below in self.corners:
                below.wait_send()


SPREAD = 20.0


def encode(values):
    return jnp.exp2(values * SPREAD).astype(jnp.bfloat16)


def decode(coded):
    return jnp.log2(coded.astype(jnp.float32)) * (1.0 / SPREAD)


def halves(values):
    high = values.astype(jnp.bfloat16)
    low = (values - high.astype(jnp.float32)).astype(jnp.bfloat16)
    return high, low


def interpolate(weight, high_block, low_block):
    rows = weight.shape[0]
    high, low = halves(weight)
    both = jnp.dot(
        jnp.concatenate([high, low], axis=0), high_block, preferred_element_type=jnp.float32
    )
    rest = both[rows:]
    if low_block is not None:
        rest = rest + jnp.dot(high, low_block, preferred_element_type=jnp.float32)
    return both[:rows] + rest


def lift(total_lon, blocks, index_ref, weight_ref, gain_ref, high_table, low_table, mesh, normed):
    @pl.loop(0, weight_ref.shape[0])
    def _(target):
        total = None
        for k in range(weight_ref.shape[1]):
            place = find_slot(index_ref[target, k], total_lon, blocks)
            term = interpolate(weight_ref[target, k], high_table[place], low_table[place])
            total = term if total is None else total + term
        mesh[target] = total
        normed[target] = layer_norm(total, gain_ref[0:1, :])


def attention(total_lon, blocks, index_ref, count_ref, queries, key_value, mixed):
    rows, width = mixed.shape[1:]
    pair = 2 * (width // HEADS)
    slots = index_ref.shape[1]
    lane = lax.broadcasted_iota(jnp.int32, (rows, pair), 1)
    first_half = lane < pair // 2
    key_block = lax.broadcasted_iota(jnp.int32, (1, slots * rows), 1) // rows

    @pl.loop(0, blocks)
    def _(target):
        live = key_block < count_ref[0, target]
        places = [find_slot(index_ref[target, s], total_lon, blocks) for s in range(slots)]

        def attend(group):
            columns = pl.ds(pl.multiple_of(group * pair, pair), pair)
            value_columns = pl.ds(pl.multiple_of(width + group * pair, pair), pair)
            query = queries[target, :, columns]
            zero = jnp.zeros_like(query)
            both = jnp.concatenate(
                [jnp.where(first_half, query, zero), jnp.where(first_half, zero, query)], axis=0
            )
            keys = jnp.concatenate([key_value[place, :, columns] for place in places], axis=0)
            values = jnp.concatenate(
                [key_value[place, :, value_columns] for place in places], axis=0
            )
            scores = lax.dot_general(
                both, keys, (((1,), (1,)), ((), ())), preferred_element_type=jnp.float32
            )
            masked = jnp.where(live, scores, -1e30)
            raw = jnp.exp(masked - jnp.max(masked, axis=-1, keepdims=True))
            total = jnp.sum(raw, axis=-1, keepdims=True)
            result = jnp.dot(
                raw.astype(jnp.bfloat16), values, preferred_element_type=jnp.float32
            ) / total
            mixed[target, :, columns] = jnp.where(
                first_half, result[:rows], result[rows:]
            ).astype(jnp.bfloat16)

        @pl.loop(0, width // pair // 2)
        def _(step):
            attend(2 * step)
            attend(2 * step + 1)


def tiled_dot(source, weight, start, end, tile, use):
    many, rows, depth = source.shape

    @pl.loop(0, (end - start) // tile)
    def _(step):
        taken = pl.ds(pl.multiple_of(start + step * tile, tile), tile)
        given = pl.ds(pl.multiple_of(step * tile, tile), tile)
        product = jnp.dot(
            source[...].reshape(many * rows, depth),
            weight[:, taken],
            preferred_element_type=jnp.float32,
        )
        use(given, product.reshape(many, rows, tile))


def layer_kernel(
    grid_lon, mesh_lon, tile,
    lift_index, window_index, window_count, return_index, grid_ref, gain_ref,
    lift_hbm, qkv_hbm, out_hbm, up_hbm, down_hbm, return_hbm,
    out_ref,
    lift_weight, qkv_weight, out_weight, up_weight, down_weight, return_weight, load_sem,
    grid_table, high_table, low_table, normed_table, mesh_table,
    mesh, normed, queries, key_value, mixed, normed_again, hidden, outgoing,
    grid_send, grid_recv, normed_send, normed_recv, mesh_send, mesh_recv,
):
    grid_blocks = grid_ref.shape[0]
    blocks, rows, width = mesh.shape
    loads = [
        pltpu.make_async_copy(source, target, load_sem.at[number])
        for number, (source, target) in enumerate(
            [
                (lift_hbm, lift_weight),
                (qkv_hbm, qkv_weight),
                (out_hbm, out_weight),
                (up_hbm, up_weight),
                (down_hbm, down_weight),
                (return_hbm, return_weight),
            ]
        )
    ]
    grid_halo = Halo(grid_ref, grid_table, grid_send, grid_recv)
    normed_halo = Halo(normed, normed_table, normed_send, normed_recv)
    mesh_halo = Halo(outgoing, mesh_table, mesh_send, mesh_recv)

    grid_halo.greet()
    grid_halo.start()
    for load in loads:
        load.start()

    def unpack(source, start, first, many):
        @pl.loop(0, many)
        def _(block):
            high, low = halves(decode(source[start + block]))
            high_table[first + block] = high
            low_table[first + block] = low

    unpack(grid_ref, 0, 0, grid_blocks)
    grid_halo.receive(grid_blocks, lambda first, many: unpack(grid_table, first, first, many))
    loads[0].wait()
    lift(
        grid_lon, grid_blocks, lift_index, lift_weight, gain_ref, high_table, low_table,
        mesh, normed,
    )
    loads[1].wait()

    normed_halo.start()
    scale = (width // HEADS) ** (-0.5)

    def keep_queries(columns, product):
        queries[:, :, columns] = product.astype(jnp.bfloat16) * jnp.bfloat16(scale)

    tiled_dot(normed, qkv_weight, 0, width, tile, keep_queries)

    def project(source, first, many):
        def keep(columns, product):
            key_value[pl.ds(first, many), :, columns] = product.astype(jnp.bfloat16)

        tiled_dot(source, qkv_weight, width, 3 * width, tile, keep)

    project(normed, 0, blocks)
    normed_halo.receive(
        blocks, lambda first, many: project(normed_table.at[pl.ds(first, many)], first, many)
    )
    attention(mesh_lon, blocks, window_index, window_count, queries, key_value, mixed)
    loads[2].wait()
    loads[3].wait()
    loads[4].wait()

    def add_mesh(columns, product):
        mesh[:, :, columns] = mesh[:, :, columns] + product

    tiled_dot(mixed, out_weight, 0, width, tile, add_mesh)
    normed_again[...] = layer_norm(mesh[...], gain_ref[1:2, :].reshape(1, 1, width))

    def keep_hidden(columns, product):
        hidden[:, :, columns] = gelu_exact(product).astype(jnp.bfloat16)

    tiled_dot(normed_again, up_weight, 0, up_weight.shape[1], tile, keep_hidden)

    def keep_outgoing(columns, product):
        value = (mesh[:, :, columns] + product).astype(jnp.bfloat16)
        outgoing[:, :, columns] = value
        mesh_table[pl.ds(0, blocks), :, columns] = value

    tiled_dot(hidden, down_weight, 0, width, tile, keep_outgoing)
    loads[5].wait()
    mesh_halo.start()
    mesh_halo.receive(blocks, lambda first, many: None)

    @pl.loop(0, return_weight.shape[0])
    def _(target):
        total = None
        for k in range(return_weight.shape[1]):
            place = find_slot(return_index[target, k], mesh_lon, blocks)
            term = interpolate(return_weight[target, k], mesh_table[place], None)
            total = term if total is None else total + term
        out_ref[target] = total

    grid_halo.finish()
    normed_halo.finish()
    mesh_halo.finish()


def in_vmem(count):
    return [pl.BlockSpec(memory_space=pltpu.VMEM)] * count


def in_smem(count):
    return [pl.BlockSpec(memory_space=pltpu.SMEM)] * count


def shards(
    grid_feats,
    lift_index,
    lift_weight,
    window_index,
    window_count,
    norm_gains,
    qkv_weight,
    out_weight,
    up_weight,
    down_weight,
    return_index,
    return_weight,
):
    lon_count = lax.axis_size("lon")
    grid_blocks = grid_feats.shape[1]
    mesh_blocks = lift_index.shape[1]
    rows = grid_feats.shape[2]
    width = grid_feats.shape[3]
    grid_lon = grid_blocks * lon_count
    mesh_lon = mesh_blocks * lon_count

    tile = min(512, width)
    hidden_width = up_weight.shape[1]
    half = jnp.bfloat16

    def table(blocks, features, held_as=half):
        return pltpu.VMEM((blocks, rows, features), held_as)

    grid_slots = 3 * (grid_blocks + 2)
    mesh_slots = 3 * (mesh_blocks + 2)
    weights = (lift_weight[0], qkv_weight, out_weight, up_weight, down_weight, return_weight[0])
    scratch = [pltpu.VMEM(weight.shape, weight.dtype) for weight in weights]
    scratch += [pltpu.SemaphoreType.DMA((len(weights),))]
    scratch += [table(grid_slots, width)] * 3 + [table(mesh_slots, width)] * 2
    scratch += [
        table(mesh_blocks, width, jnp.float32),
        table(mesh_blocks, width),
        table(mesh_blocks, width),
        table(mesh_slots, 2 * width),
        table(mesh_blocks, width),
        table(mesh_blocks, width),
        table(mesh_blocks, hidden_width),
        table(mesh_blocks, width),
    ]
    for blocks in (grid_blocks, mesh_blocks, mesh_blocks):
        scratch += [pltpu.SemaphoreType.DMA((Halo.count(blocks),))] * 2
    grid_out = pl.pallas_call(
        lambda *refs: layer_kernel(grid_lon, mesh_lon, tile, *refs),
        out_shape=jax.ShapeDtypeStruct((grid_blocks, rows, width), jnp.float32),
        in_specs=in_smem(4)
        + in_vmem(2)
        + [pl.BlockSpec(memory_space=pl.ANY)] * len(weights),
        out_specs=in_vmem(1)[0],
        scratch_shapes=scratch,
        compiler_params=pltpu.CompilerParams(
            collective_id=0, has_side_effects=True, vmem_limit_bytes=VMEM_LIMIT
        ),
    )(
        lift_index[0],
        window_index[0],
        window_count,
        return_index[0],
        encode(grid_feats[0]),
        norm_gains,
        *weights,
    )
    return grid_out.reshape(1, grid_blocks, rows, width)


def solution(mesh):
    placed = (
        P("lat", "lon", None, None),
        P("lat", "lon", None),
        P("lat", "lon", None, None, None),
        P("lat", "lon", None),
        P("lat", "lon"),
        P(),
        P(),
        P(),
        P(),
        P(),
        P("lat", "lon", None),
        P("lat", "lon", None, None, None),
    )
    return jax.shard_map(
        shards, mesh=mesh, in_specs=placed, out_specs=P("lat", "lon", None, None), check_vma=False
    )
```

```python
import jax
import jax.numpy as jnp
from jax import lax
from jax.experimental import pallas as pl
from jax.experimental.pallas import tpu as pltpu
from jax.sharding import PartitionSpec as P

HEADS = 16


EPSILON = 1e-05

MESH = pl.DeviceIdType.MESH
VMEM_LIMIT = 60 * 1024 * 1024


def layer_norm(values, gain):
    centred = values - jnp.mean(values, axis=-1, keepdims=True)
    spread = jnp.mean(centred * centred, axis=-1, keepdims=True)
    return (centred * lax.rsqrt(spread + EPSILON) * gain).astype(jnp.bfloat16)


def gelu_exact(values):
    return 0.5 * values * (1.0 + lax.erf(values * 0.7071067811865476))


def find_slot(global_id, total_lon, blocks):
    sector_here = lax.axis_index("lon")
    odd = lax.rem(sector_here, 2)
    source_band = lax.div(global_id, total_lon)
    row = source_band - lax.axis_index("lat")
    column = lax.rem(
        global_id - source_band * total_lon - sector_here * blocks + 1 + total_lon, total_lon
    )
    band = jnp.where(row < 0, 0, 1)
    place = column - 1
    side = jnp.where(column == 0, 0, 1)
    outside = jnp.logical_or(column == 0, column == blocks + 1)
    first = odd * (blocks - 1)
    corner = jnp.where(side == odd, blocks + 8 + 2 * (blocks - 2) + band, blocks + 6 + band)
    border = jnp.where(place == first, blocks + 2 + band, blocks + 4 + band)
    between = blocks + 8 + band * (blocks - 2) + place - 1
    middle = jnp.logical_and(place > 0, place < blocks - 1)
    other = jnp.where(outside, corner, jnp.where(middle, between, border))
    same = jnp.where(outside, blocks + side, place)
    found = jnp.where(row == 0, same, other)
    return jnp.minimum(jnp.maximum(found, 0), 3 * (blocks + 2) - 1)


class Halo:
    def __init__(self, source, table, send_sem, recv_sem):
        blocks = source.shape[0]
        lat_count, lon_count = lax.axis_size("lat"), lax.axis_size("lon")
        lat, lon = lax.axis_index("lat"), lax.axis_index("lon")
        odd = lax.rem(lon, 2)
        self.above, self.below = lat > 0, lat < lat_count - 1
        self.outer = (lat, lax.rem(lon + 2 * odd - 1 + lon_count, lon_count))
        self.inner = (lat, lax.rem(lon + 1 - 2 * odd + lon_count, lon_count))
        self.down = (lax.rem(lat + 1, lat_count), lon)
        self.up = (lax.rem(lat + lat_count - 1, lat_count), lon)
        first = odd * (blocks - 1)
        second = blocks - 1 - first
        number = 0

        def copy(src, dst, device):
            nonlocal number
            number += 1
            return pltpu.make_async_remote_copy(
                src_ref=src,
                dst_ref=dst,
                send_sem=send_sem.at[number - 1],
                recv_sem=recv_sem.at[number - 1],
                device_id=device,
                device_id_type=MESH,
            )

        self.edges = [
            copy(source.at[first], table.at[blocks + 1 - odd], self.outer),
            copy(source.at[second], table.at[blocks + odd], self.inner),
        ]
        piece = source.shape[1] // 2
        pieces = [pl.ds(0, piece), pl.ds(piece, piece)]
        self.vertical = []
        for part in pieces:
            self.vertical.append(
                (
                    copy(source.at[first, part], table.at[blocks + 2, part], self.down),
                    copy(source.at[first, part], table.at[blocks + 3, part], self.up),
                )
            )
        self.vertical.append(
            (
                copy(source.at[second], table.at[blocks + 4], self.down),
                copy(source.at[second], table.at[blocks + 5], self.up),
            )
        )
        between = blocks + 8
        for place in range(1, blocks - 1):
            slot = between + place - 1
            self.vertical.append(
                (
                    copy(source.at[place], table.at[slot], self.down),
                    copy(source.at[place], table.at[slot + blocks - 2], self.up),
                )
            )
        last = between + 2 * (blocks - 2)
        self.corners = [
            [
                copy(table.at[blocks + 2 + band, part], table.at[last + band, part], self.outer)
                for band in (0, 1)
            ]
            for part in pieces
        ] + [
            [
                copy(table.at[blocks + 4 + band], table.at[blocks + 6 + band], self.inner)
                for band in (0, 1)
            ],
        ]

    @staticmethod
    def count(blocks):
        return 10 + 2 * blocks

    def greet(self):
        barrier = pltpu.get_barrier_semaphore()
        for device in (self.outer, self.inner):
            pl.semaphore_signal(barrier, inc=1, device_id=device, device_id_type=MESH)

        @pl.when(self.above)
        def _():
            pl.semaphore_signal(barrier, inc=1, device_id=self.up, device_id_type=MESH)

        @pl.when(self.below)
        def _():
            pl.semaphore_signal(barrier, inc=1, device_id=self.down, device_id_type=MESH)

        bands = self.above.astype(jnp.int32) + self.below.astype(jnp.int32)
        pl.semaphore_wait(barrier, 2 + bands)

    def start(self):
        for edge in self.edges[:1]:
            edge.start()
        for down, up in self.vertical:
            @pl.when(self.below)
            def _():
                down.start()

            @pl.when(self.above)
            def _():
                up.start()
        for edge in self.edges[1:]:
            edge.start()

    def forward(self, order):
        down, up = self.vertical[order]
        above, below = self.corners[order]

        @pl.when(self.above)
        def _():
            down.wait_recv()
            above.start()

        @pl.when(self.below)
        def _():
            up.wait_recv()
            below.start()

    def wait_edges(self):
        for edge in self.edges:
            edge.wait_recv()

    def wait_corners(self, order):
        above, below = self.corners[order]

        @pl.when(self.above)
        def _():
            above.wait_recv()

        @pl.when(self.below)
        def _():
            below.wait_recv()

    def wait_between(self):
        for down, up in self.vertical[3:]:
            @pl.when(self.above)
            def _():
                down.wait_recv()

            @pl.when(self.below)
            def _():
                up.wait_recv()

    def receive(self, blocks, work):
        self.forward(1)
        self.wait_edges()
        work(blocks, 4)
        self.forward(2)
        self.wait_corners(2)
        work(blocks + 4, 4)
        self.wait_between()
        self.wait_corners(0)
        self.wait_corners(1)
        work(blocks + 8, 2 * (blocks - 2) + 2)

    def finish(self):
        for edge in self.edges:
            edge.wait_send()

        @pl.when(self.above)
        def _():
            for _, up in self.vertical:
                up.wait_send()
            for above, _ in self.corners:
                above.wait_send()

        @pl.when(self.below)
        def _():
            for down, _ in self.vertical:
                down.wait_send()
            for _, below in self.corners:
                below.wait_send()


SPREAD = 20.0


def encode(values):
    return jnp.exp2(values * SPREAD).astype(jnp.bfloat16)


def decode(coded):
    return jnp.log2(coded.astype(jnp.float32)) * (1.0 / SPREAD)


def halves(values):
    high = values.astype(jnp.bfloat16)
    low = (values - high.astype(jnp.float32)).astype(jnp.bfloat16)
    return high, low


def interpolate(weight, high_block, low_block):
    rows = weight.shape[0]
    high, low = halves(weight)
    both = jnp.dot(
        jnp.concatenate([high, low], axis=0), high_block, preferred_element_type=jnp.float32
    )
    rest = both[rows:]
    if low_block is not None:
        rest = rest + jnp.dot(high, low_block, preferred_element_type=jnp.float32)
    return both[:rows] + rest


def lift(total_lon, blocks, index_ref, weight_ref, gain_ref, high_table, low_table, mesh, normed):
    @pl.loop(0, weight_ref.shape[0])
    def _(target):
        total = None
        for k in range(weight_ref.shape[1]):
            place = find_slot(index_ref[target, k], total_lon, blocks)
            term = interpolate(weight_ref[target, k], high_table[place], low_table[place])
            total = term if total is None else total + term
        mesh[target] = total
        normed[target] = layer_norm(total, gain_ref[0:1, :])


def attention(total_lon, blocks, skip, index_ref, count_ref, queries, key_value, mixed):
    rows, width = mixed.shape[1:]
    pair = 2 * (width // HEADS)
    slots = index_ref.shape[1] - skip
    lane = lax.broadcasted_iota(jnp.int32, (rows, pair), 1)
    first_half = lane < pair // 2
    key_block = lax.broadcasted_iota(jnp.int32, (1, slots * rows), 1) // rows

    @pl.loop(0, blocks)
    def _(target):
        live = key_block < count_ref[0, target]
        places = [find_slot(index_ref[target, skip + s], total_lon, blocks) for s in range(slots)]

        def attend(group):
            columns = pl.ds(pl.multiple_of(group * pair, pair), pair)
            value_columns = pl.ds(pl.multiple_of(width + group * pair, pair), pair)
            query = queries[target, :, columns]
            zero = jnp.zeros_like(query)
            both = jnp.concatenate(
                [jnp.where(first_half, query, zero), jnp.where(first_half, zero, query)], axis=0
            )
            keys = jnp.concatenate([key_value[place, :, columns] for place in places], axis=0)
            values = jnp.concatenate(
                [key_value[place, :, value_columns] for place in places], axis=0
            )
            scores = lax.dot_general(
                both, keys, (((1,), (1,)), ((), ())), preferred_element_type=jnp.float32
            )
            masked = jnp.where(live, scores, -1e30)
            raw = jnp.exp(masked - jnp.max(masked, axis=-1, keepdims=True))
            total = jnp.sum(raw, axis=-1, keepdims=True)
            result = jnp.dot(
                raw.astype(jnp.bfloat16), values, preferred_element_type=jnp.float32
            ) / total
            mixed[target, :, columns] = jnp.where(
                first_half, result[:rows], result[rows:]
            ).astype(jnp.bfloat16)

        @pl.loop(0, width // pair // 2)
        def _(step):
            attend(2 * step)
            attend(2 * step + 1)


def tiled_dot(source, weight, start, end, tile, use):
    many, rows, depth = source.shape

    @pl.loop(0, (end - start) // tile)
    def _(step):
        taken = pl.ds(pl.multiple_of(start + step * tile, tile), tile)
        given = pl.ds(pl.multiple_of(step * tile, tile), tile)
        product = jnp.dot(
            source[...].reshape(many * rows, depth),
            weight[:, taken],
            preferred_element_type=jnp.float32,
        )
        use(given, product.reshape(many, rows, tile))


def layer_kernel(
    grid_lon, mesh_lon, tile,
    mesh_index, window_count, return_index, grid_ref, gain_ref,
    lift_hbm, qkv_hbm, out_hbm, up_hbm, down_hbm, return_hbm,
    out_ref,
    lift_weight, qkv_weight, out_weight, up_weight, down_weight, return_weight, load_sem,
    grid_table, high_table, low_table, normed_table, mesh_table,
    mesh, normed, queries, key_value, mixed, normed_again, hidden, outgoing,
    grid_send, grid_recv, normed_send, normed_recv, mesh_send, mesh_recv,
):
    grid_blocks = grid_ref.shape[0]
    blocks, rows, width = mesh.shape
    loads = [
        pltpu.make_async_copy(source, target, load_sem.at[number])
        for number, (source, target) in enumerate(
            [
                (lift_hbm, lift_weight),
                (qkv_hbm, qkv_weight),
                (out_hbm, out_weight),
                (up_hbm, up_weight),
                (down_hbm, down_weight),
                (return_hbm, return_weight),
            ]
        )
    ]
    grid_halo = Halo(grid_ref, grid_table, grid_send, grid_recv)
    normed_halo = Halo(normed, normed_table, normed_send, normed_recv)
    mesh_halo = Halo(outgoing, mesh_table, mesh_send, mesh_recv)

    grid_halo.greet()
    grid_halo.start()
    for load in loads:
        load.start()

    def unpack(source, start, first, many):
        @pl.loop(0, many)
        def _(block):
            high, low = halves(decode(source[start + block]))
            high_table[first + block] = high
            low_table[first + block] = low

    grid_halo.forward(0)
    unpack(grid_ref, 0, 0, grid_blocks)
    grid_halo.receive(grid_blocks, lambda first, many: unpack(grid_table, first, first, many))
    loads[0].wait()
    lift(
        grid_lon, grid_blocks, mesh_index, lift_weight, gain_ref, high_table, low_table,
        mesh, normed,
    )
    loads[1].wait()

    normed_halo.start()
    scale = (width // HEADS) ** (-0.5)

    def keep_queries(columns, product):
        queries[:, :, columns] = product.astype(jnp.bfloat16) * jnp.bfloat16(scale)

    tiled_dot(normed, qkv_weight, 0, width, tile, keep_queries)

    def project(source, first, many):
        def keep(columns, product):
            key_value[pl.ds(first, many), :, columns] = product.astype(jnp.bfloat16)

        tiled_dot(source, qkv_weight, width, 3 * width, tile, keep)

    normed_halo.forward(0)
    project(normed, 0, blocks)
    normed_halo.receive(
        blocks, lambda first, many: project(normed_table.at[pl.ds(first, many)], first, many)
    )
    attention(mesh_lon, blocks, lift_weight.shape[1], mesh_index, window_count, queries, key_value, mixed)
    loads[2].wait()
    loads[3].wait()
    loads[4].wait()

    def add_mesh(columns, product):
        mesh[:, :, columns] = mesh[:, :, columns] + product

    tiled_dot(mixed, out_weight, 0, width, tile, add_mesh)
    normed_again[...] = layer_norm(mesh[...], gain_ref[1:2, :].reshape(1, 1, width))

    def keep_hidden(columns, product):
        hidden[:, :, columns] = gelu_exact(product).astype(jnp.bfloat16)

    tiled_dot(normed_again, up_weight, 0, up_weight.shape[1], tile, keep_hidden)

    def keep_outgoing(columns, product):
        value = (mesh[:, :, columns] + product).astype(jnp.bfloat16)
        outgoing[:, :, columns] = value
        mesh_table[pl.ds(0, blocks), :, columns] = value

    tiled_dot(hidden, down_weight, 0, width, tile, keep_outgoing)
    loads[5].wait()
    mesh_halo.start()
    mesh_halo.forward(0)
    mesh_halo.receive(blocks, lambda first, many: None)

    @pl.loop(0, return_weight.shape[0])
    def _(target):
        total = None
        for k in range(return_weight.shape[1]):
            place = find_slot(return_index[target, k], mesh_lon, blocks)
            term = interpolate(return_weight[target, k], mesh_table[place], None)
            total = term if total is None else total + term
        out_ref[target] = total

    grid_halo.finish()
    normed_halo.finish()
    mesh_halo.finish()


def in_vmem(count):
    return [pl.BlockSpec(memory_space=pltpu.VMEM)] * count


def in_smem(count):
    return [pl.BlockSpec(memory_space=pltpu.SMEM)] * count


def shards(
    grid_feats,
    lift_index,
    lift_weight,
    window_index,
    window_count,
    norm_gains,
    qkv_weight,
    out_weight,
    up_weight,
    down_weight,
    return_index,
    return_weight,
):
    lon_count = lax.axis_size("lon")
    grid_blocks = grid_feats.shape[1]
    mesh_blocks = lift_index.shape[1]
    rows = grid_feats.shape[2]
    width = grid_feats.shape[3]
    grid_lon = grid_blocks * lon_count
    mesh_lon = mesh_blocks * lon_count

    tile = min(512, width)
    hidden_width = up_weight.shape[1]
    half = jnp.bfloat16

    def table(blocks, features, held_as=half):
        return pltpu.VMEM((blocks, rows, features), held_as)

    grid_slots = 3 * (grid_blocks + 2)
    mesh_slots = 3 * (mesh_blocks + 2)
    weights = (lift_weight[0], qkv_weight, out_weight, up_weight, down_weight, return_weight[0])
    scratch = [pltpu.VMEM(weight.shape, weight.dtype) for weight in weights]
    scratch += [pltpu.SemaphoreType.DMA((len(weights),))]
    scratch += [table(grid_slots, width)] * 3 + [table(mesh_slots, width)] * 2
    scratch += [
        table(mesh_blocks, width, jnp.float32),
        table(mesh_blocks, width),
        table(mesh_blocks, width),
        table(mesh_slots, 2 * width),
        table(mesh_blocks, width),
        table(mesh_blocks, width),
        table(mesh_blocks, hidden_width),
        table(mesh_blocks, width),
    ]
    for blocks in (grid_blocks, mesh_blocks, mesh_blocks):
        scratch += [pltpu.SemaphoreType.DMA((Halo.count(blocks),))] * 2
    grid_out = pl.pallas_call(
        lambda *refs: layer_kernel(grid_lon, mesh_lon, tile, *refs),
        out_shape=jax.ShapeDtypeStruct((grid_blocks, rows, width), jnp.float32),
        in_specs=in_smem(3)
        + in_vmem(2)
        + [pl.BlockSpec(memory_space=pl.ANY)] * len(weights),
        out_specs=in_vmem(1)[0],
        scratch_shapes=scratch,
        compiler_params=pltpu.CompilerParams(
            collective_id=0, has_side_effects=True, vmem_limit_bytes=VMEM_LIMIT
        ),
    )(
        jnp.concatenate([lift_index[0], window_index[0]], axis=-1),
        window_count,
        return_index[0],
        encode(grid_feats[0]),
        norm_gains,
        *weights,
    )
    return grid_out.reshape(1, grid_blocks, rows, width)


def solution(mesh):
    placed = (
        P("lat", "lon", None, None),
        P("lat", "lon", None),
        P("lat", "lon", None, None, None),
        P("lat", "lon", None),
        P("lat", "lon"),
        P(),
        P(),
        P(),
        P(),
        P(),
        P("lat", "lon", None),
        P("lat", "lon", None, None, None),
    )
    return jax.shard_map(
        shards, mesh=mesh, in_specs=placed, out_specs=P("lat", "lon", None, None), check_vma=False
    )
```
